32 devices in a mesh: groups: 2 (over y), chol: 4 (over z), walk: 4 (over x, core).
Axes of the slice: x: 2, y: 2, z: 4, core: 2. Of those that a mesh axis runs over, the one named last changes fastest.
Arguments:
- green: bfloat16 [8, 200, 1600], P(('groups', 'walk')), parts along dimension 0, may hold values from -2 to 2
- chol: bfloat16 [16, 200, 1600], P(('groups', 'chol')), parts along dimension 0, may hold values from -0.19921875 to 0.19921875
- trial: bfloat16 [3200, 200], P(('groups', 'chol')), parts along dimension 0, may hold values from -1.1953125 to 1.1953125
- hamil: bfloat16 [1600, 1600], P('chol'), may hold values from -0.21875 to 0.21875
- energy_cot: float32 [8], P('groups'), parts along dimension 0, may hold values from -4 to 4
Outputs:
- d_green: float32 [8, 200, 1600], P(('groups', 'walk'), None, 'chol'), parts along dimension 0
- d_chol: float32 [16, 200, 1600], P(('groups', 'chol'), None, 'walk'), parts along dimension 0
- d_trial: float32 [3200, 200], P(('groups', 'chol')), parts along dimension 0
The draws below stay inside these ranges and needn't reach their ends.
There are 2 independent parts, one for each index of `groups`. The reference program is written for one: setup_inputs(seed, part) draws one part's arguments, and reference() takes and returns one part's arrays. A program takes and returns all parts, laid end to end along the dimension named above; an argument that names none is the same for every part. Nothing has to cross between parts.
All inputs are finite; a program needn't handle non-finite values.
Results may differ from the reference program's by a relative error of at most 0.0029.
Values may be sent and summed in bfloat16 or wider, within the bound.
No kernel may reach another device: no remote copies, remote signals or barrier semaphores. Data moves between devices by JAX's collectives and lax.ppermute only.
A program may use at most 64 MiB of HBM per device.

```python
import jax
import jax.numpy as jnp
from jax import lax

NOCC = 200
NORB = 1600
NCHOL = 8
NWALK = 4


def raised(result, own_key, source, target, blocks, factor):
    owner, partner = [(jnp.arange(result.shape[position]) // (result.shape[position] // blocks)).reshape([-1 if axis == position else 1 for axis in range(result.ndim)]) for position in (source, target)]
    chosen = jax.random.permutation(own_key, blocks)[partner]
    strong = (owner == chosen) | (owner == (partner + blocks // 2) % blocks)
    return jnp.where(strong, factor * result, result)


def block_scale(rng, dims, pieces, low, largest):
    def one(position, shards_of):
        heights = jax.random.uniform(jax.random.fold_in(jax.random.fold_in(rng, 6), position), (shards_of,), jnp.float32, low / len(pieces), largest / len(pieces))
        return jnp.repeat(jnp.exp(heights), dims[position] // shards_of).reshape((-1,) + (1,) * (len(dims) - position - 1))

    level = one(*pieces[0])
    for cut in pieces[1:]:
        level = level * one(*cut)
    return level


def centred(rng, extent, deviation, limit, cuts=(), kind=jnp.bfloat16):
    array = jax.random.normal(rng, extent, jnp.float32) * deviation
    if len(cuts) > 0:
        array = block_scale(rng, extent, cuts, -0.22, 0.18) * array
    return jnp.clip(array, min=-limit, max=limit).astype(kind)


def bell_draw_with(key, shape, width, most, cuts, heavy, kind=jnp.bfloat16):
    array = width * jax.random.normal(key, shape, jnp.float32)
    if cuts:
        array = array * block_scale(key, shape, cuts, -0.22, 0.18)
    return jnp.clip(raised(array, jax.random.fold_in(key, 3), *heavy), -most, most).astype(kind)


def setup_inputs(seed: int = 0, part: int = 0) -> dict:
    key_of = jax.random.split(jax.random.key(seed), 6)
    part_splits = jax.random.split(jax.random.fold_in(key_of[5], part), 6)
    green = centred(part_splits[0], (NWALK, NOCC, NORB), 0.3, 2.0, ((0, 4),))
    chol = bell_draw_with(part_splits[1], (NCHOL, NOCC, NORB), 0.02, 0.19921875, ((0, 4),), (0, 2, 4, 2.0))
    trial = centred(part_splits[2], (NORB, NOCC), 0.2, 1.1953125, ((0, 4),))
    hamil = bell_draw_with(key_of[3], (NORB, NORB), NORB ** -0.5, 0.21875, ((0, 4),), (0, 1, 4, 2.0))
    energy_cot = centred(part_splits[4], (NWALK,), 1.0, 4.0, (), jnp.float32)
    return dict(green=green, chol=chol, trial=trial, hamil=hamil, energy_cot=energy_cot)


def reference(green, chol, trial, hamil, energy_cot):
    green_f32 = green.astype(jnp.float32)
    hrot = jnp.dot(trial.T, hamil, preferred_element_type=jnp.float32)
    identity = jnp.eye(NOCC, dtype=jnp.float32)

    def accumulate(total, slab_vec):
        slab_f32 = slab_vec.astype(jnp.float32)
        coulomb = jnp.einsum("wip,ip->w", green_f32, slab_f32)
        exchange_mat = jnp.einsum("ip,wjp->wij", slab_f32, green_f32)
        kernel_mat = (energy_cot[:, None, None] * (coulomb[:, None, None] * identity - exchange_mat)).astype(jnp.bfloat16)
        kernel_f32 = lax.optimization_barrier(kernel_mat).astype(jnp.float32)
        slab_grad = jnp.einsum("wji,wjp->ip", kernel_f32, green_f32)
        total = total + jnp.einsum("wij,jp->wip", kernel_f32, slab_f32)
        return total, slab_grad

    start_total = energy_cot[:, None, None] * hrot[None]
    d_green, d_chol = lax.scan(accumulate, start_total, chol)
    gbar = jnp.einsum("w,wip->ip", energy_cot, green_f32, precision=lax.Precision.HIGHEST).astype(jnp.bfloat16)
    d_trial = jnp.dot(hamil, gbar.T, preferred_element_type=jnp.float32)
    return d_green, d_chol, d_trial
```

```python
import functools

import jax
import jax.numpy as jnp
from jax import lax
from jax.experimental import pallas as pl
from jax.experimental.pallas import tpu as pltpu
from jax.sharding import PartitionSpec as P


F32 = jnp.float32
BF16 = jnp.bfloat16
LANES = 128
SUBLANES = 8
MIB = 1024 * 1024


def plain(green, chol, trial, hamil, energy_cot):
    walk_rank = lax.axis_index("walk")
    walk_rows = green.shape[0]
    cot_own = lax.dynamic_slice_in_dim(energy_cot, walk_rank * walk_rows, walk_rows, 0)
    hrot_part = lax.dot_general(
        trial, hamil, (((0,), (0,)), ((), ())), preferred_element_type=F32
    )
    identity = jnp.eye(trial.shape[1], dtype=F32)
    quarter = green.shape[2] // lax.axis_size("walk")
    greens = lax.all_gather(green, "walk", axis=0, tiled=True)
    coulomb = jnp.einsum("cip,wip->cw", chol, greens, preferred_element_type=F32)
    exchange_mat = jnp.einsum("cip,wjp->cwij", chol, greens, preferred_element_type=F32)
    kernel_mat = (
        energy_cot[None, :, None, None] * (coulomb[:, :, None, None] * identity - exchange_mat)
    ).astype(BF16)
    kernel_own = lax.dynamic_slice_in_dim(kernel_mat, walk_rank * walk_rows, walk_rows, 1)
    green_part = jnp.einsum("cwij,cjp->wip", kernel_own, chol, preferred_element_type=F32)
    green_part = green_part + cot_own[:, None, None] * hrot_part[None]
    d_green = lax.psum_scatter(green_part, "chol", scatter_dimension=2, tiled=True)
    green_share = lax.dynamic_slice_in_dim(greens, walk_rank * quarter, quarter, 2)
    d_chol = jnp.einsum("cwji,wjp->cip", kernel_mat, green_share, preferred_element_type=F32)
    gbar = jnp.einsum(
        "w,wip->ip",
        energy_cot,
        greens,
        precision=lax.Precision.HIGHEST,
        preferred_element_type=F32,
    ).astype(BF16)
    d_trial = lax.dot_general(hamil, gbar, (((1,), (1,)), ((), ())), preferred_element_type=F32)
    return (d_green, d_chol, d_trial)


def nn(a, b):
    return jnp.dot(a, b, preferred_element_type=F32)


def nt(a, b):
    return lax.dot_general(a, b, (((1,), (1,)), ((), ())), preferred_element_type=F32)


def kernel_of(exch, cot):
    row = lax.broadcasted_iota(jnp.int32, exch.shape, 0)
    col = lax.broadcasted_iota(jnp.int32, exch.shape, 1)
    on_diagonal = jnp.where(row == col, exch, 0.0)
    coul = jnp.sum(jnp.sum(on_diagonal, axis=0, keepdims=True), axis=1, keepdims=True)
    return (cot * (jnp.where(row == col, coul, 0.0) - exch)).astype(BF16)


def row_groups(rows, width):
    fits = [n for n in range(1, rows + 1) if rows % n == 0 and rows // n % SUBLANES == 0]
    padded = {n: -(-n * width // LANES) * LANES / n for n in fits}
    least = min(padded.values())
    return min(n for n in fits if padded[n] <= 1.03 * least)


def partials_kernel(blocks, groups, cot_ref, green_ref, chol_ref, trial_ref, hamil_ref, *refs):
    outs, own_ref, part_ref, packed_ref = refs[: blocks - 1], *refs[blocks - 1 :]
    rank = lax.axis_index("chol")
    cot = cot_ref[lax.axis_index("walk")]
    green = green_ref[0]
    nocc, norb = green.shape
    width = norb // blocks
    height = nocc // groups
    total = cot * nn(trial_ref[...].T, hamil_ref[...])
    for v in range(chol_ref.shape[0]):
        vector = chol_ref[v]
        total += nn(kernel_of(nt(vector, green), cot), vector)
    part_ref[...] = total
    for q in range(blocks):
        for r in range(groups):
            packed_ref[q, :, r * width : (r + 1) * width] = part_ref[
                r * height : (r + 1) * height, q * width : (q + 1) * width
            ]
    for k in range(1, blocks):
        outs[k - 1][...] = packed_ref[rank ^ k].astype(BF16)
    own_ref[...] = packed_ref[rank]


def partials(blocks, groups, green, chol, trial, hamil, cot):
    _, nocc, norb = green.shape
    block = (nocc // groups, groups * (norb // blocks))
    vmem = pl.BlockSpec(memory_space=pltpu.VMEM)
    return pl.pallas_call(
        functools.partial(partials_kernel, blocks, groups),
        out_shape=[jax.ShapeDtypeStruct(block, BF16)] * (blocks - 1)
        + [jax.ShapeDtypeStruct(block, F32)],
        in_specs=[pl.BlockSpec(memory_space=pltpu.SMEM)] + [vmem] * 4,
        out_specs=[vmem] * blocks,
        scratch_shapes=[
            pltpu.VMEM((nocc, norb), F32),
            pltpu.VMEM((blocks,) + block, F32),
        ],
        cost_estimate=pl.CostEstimate(
            flops=2 * nocc * norb * (2 * chol.shape[0] * nocc + trial.shape[0]),
            bytes_accessed=2 * (green.size + chol.size + trial.size + hamil.size + 5 * nocc * norb // 4),
            transcendentals=0,
        ),
        compiler_params=pltpu.CompilerParams(vmem_limit_bytes=16 * MIB),
        name="partials",
    )(cot, green, chol, trial, hamil)


def walkers_kernel(order, last, ways, cot_ref, chol_ref, hamil_ref, *refs):
    count = len(order)
    greens, refs = refs[:count], refs[count:]
    if last:
        old_chol, old_bar, d_chol_ref, d_trial_ref, share = refs
    else:
        d_chol_ref, bar_ref, share = refs
    rank = lax.axis_index("walk")
    width = share.shape[2]
    for place in range(ways):

        @pl.when(rank == place)
        def _():
            for n in range(count):
                share[n] = greens[n][0, :, place * width : (place + 1) * width]

    bar = old_bar[...] if last else 0.0
    for n in range(count):
        bar += cot_ref[rank ^ order[n]] * greens[n][0].astype(F32)
    if last:
        d_trial_ref[...] = nt(hamil_ref[...], bar.astype(BF16))
    else:
        bar_ref[...] = bar
    for v in range(chol_ref.shape[0]):
        total = old_chol[v] if last else 0.0
        for n in range(count):
            flipped = nt(greens[n][0], chol_ref[v])
            total += nn(kernel_of(flipped, cot_ref[rank ^ order[n]]), share[n])
        d_chol_ref[v] = total


def walkers(order, last, ways, cot, chol, hamil, greens, old=()):
    vectors, nocc, norb = chol.shape
    width = norb // ways
    vmem = pl.BlockSpec(memory_space=pltpu.VMEM)
    second = (hamil.shape[0], nocc) if last else (nocc, norb)
    return pl.pallas_call(
        functools.partial(walkers_kernel, order, last, ways),
        out_shape=[
            jax.ShapeDtypeStruct((vectors, nocc, width), F32),
            jax.ShapeDtypeStruct(second, F32),
        ],
        in_specs=[pl.BlockSpec(memory_space=pltpu.SMEM)] + [vmem] * (2 + len(greens) + len(old)),
        out_specs=[vmem] * 2,
        scratch_shapes=[pltpu.VMEM((len(order), nocc, width), BF16)],
        cost_estimate=pl.CostEstimate(
            flops=2 * nocc * nocc * vectors * len(order) * (norb + width)
            + (2 * hamil.size * nocc if last else 0),
            bytes_accessed=2 * (chol.size + hamil.size + len(order) * nocc * norb),
            transcendentals=0,
        ),
        compiler_params=pltpu.CompilerParams(vmem_limit_bytes=16 * MIB),
        name="walkers_last" if last else "walkers_first",
    )(cot, chol, hamil, *greens, *old)


def joined_kernel(groups, own_ref, *refs):
    received, out_ref, sum_ref = refs[:-2], refs[-2], refs[-1]
    total = own_ref[...]
    for part in received:
        total += part[...].astype(F32)
    sum_ref[...] = total
    height = total.shape[0]
    width = total.shape[1] // groups
    for r in range(groups):
        out_ref[0, r * height : (r + 1) * height, :] = sum_ref[:, r * width : (r + 1) * width]


def joined(groups, own, received):
    height, long = own.shape
    vmem = pl.BlockSpec(memory_space=pltpu.VMEM)
    return pl.pallas_call(
        functools.partial(joined_kernel, groups),
        out_shape=jax.ShapeDtypeStruct((1, groups * height, long // groups), F32),
        in_specs=[vmem] * (1 + len(received)),
        out_specs=vmem,
        scratch_shapes=[pltpu.VMEM((height, long), F32)],
        cost_estimate=pl.CostEstimate(
            flops=own.size * 4, bytes_accessed=own.size * 16, transcendentals=0
        ),
        compiler_params=pltpu.CompilerParams(vmem_limit_bytes=16 * MIB),
        name="joined",
    )(own, *received)


def swapped(x, axis, bits):
    return lax.ppermute(x, axis, [(i, i ^ bits) for i in range(lax.axis_size(axis))])


def shards(green, chol, trial, hamil, energy_cot):
    ways = lax.axis_size("walk")
    blocks = lax.axis_size("chol")
    _, nocc, norb = green.shape
    groups = row_groups(nocc, norb // blocks)
    far = swapped(green, "walk", 2)
    near = swapped(green, "walk", 1)
    *away, own = partials(blocks, groups, green, chol, trial, hamil, energy_cot)
    received = [swapped(block, "chol", k + 1) for k, block in enumerate(away)]
    first = walkers((0, 1), False, ways, energy_cot, chol, hamil, [green, near])
    other = swapped(far, "walk", 1)
    d_chol, d_trial = walkers((2, 3), True, ways, energy_cot, chol, hamil, [far, other], first)
    d_green = joined(groups, own, received)
    return (d_green, d_chol, d_trial)


def solution(mesh):
    fits = mesh.shape["walk"] == 4 and mesh.shape["chol"] in (2, 4)

    def body(green, *rest):
        if fits and green.shape[0] == 1 and green.shape[1] % SUBLANES == 0:
            return shards(green, *rest)
        return plain(green, *rest)

    return jax.shard_map(
        body,
        mesh=mesh,
        in_specs=(
            P(("groups", "walk"), None, None),
            P(("groups", "chol"), None, None),
            P(("groups", "chol"), None),
            P("chol", None),
            P("groups"),
        ),
        out_specs=(
            P(("groups", "walk"), None, "chol"),
            P(("groups", "chol"), None, "walk"),
            P(("groups", "chol"), None),
        ),
        check_vma=False,
    )
```

```python
import functools

import jax
import jax.numpy as jnp
from jax import lax
from jax.experimental import pallas as pl
from jax.experimental.pallas import tpu as pltpu
from jax.sharding import PartitionSpec as P


F32 = jnp.float32
BF16 = jnp.bfloat16
LANES = 128
SUBLANES = 8
MIB = 1024 * 1024


def plain(green, chol, trial, hamil, energy_cot):
    walk_rank = lax.axis_index("walk")
    walk_rows = green.shape[0]
    cot_own = lax.dynamic_slice_in_dim(energy_cot, walk_rank * walk_rows, walk_rows, 0)
    hrot_part = lax.dot_general(
        trial, hamil, (((0,), (0,)), ((), ())), preferred_element_type=F32
    )
    identity = jnp.eye(trial.shape[1], dtype=F32)
    quarter = green.shape[2] // lax.axis_size("walk")
    greens = lax.all_gather(green, "walk", axis=0, tiled=True)
    coulomb = jnp.einsum("cip,wip->cw", chol, greens, preferred_element_type=F32)
    exchange_mat = jnp.einsum("cip,wjp->cwij", chol, greens, preferred_element_type=F32)
    kernel_mat = (
        energy_cot[None, :, None, None] * (coulomb[:, :, None, None] * identity - exchange_mat)
    ).astype(BF16)
    kernel_own = lax.dynamic_slice_in_dim(kernel_mat, walk_rank * walk_rows, walk_rows, 1)
    green_part = jnp.einsum("cwij,cjp->wip", kernel_own, chol, preferred_element_type=F32)
    green_part = green_part + cot_own[:, None, None] * hrot_part[None]
    d_green = lax.psum_scatter(green_part, "chol", scatter_dimension=2, tiled=True)
    green_share = lax.dynamic_slice_in_dim(greens, walk_rank * quarter, quarter, 2)
    d_chol = jnp.einsum("cwji,wjp->cip", kernel_mat, green_share, preferred_element_type=F32)
    gbar = jnp.einsum(
        "w,wip->ip",
        energy_cot,
        greens,
        precision=lax.Precision.HIGHEST,
        preferred_element_type=F32,
    ).astype(BF16)
    d_trial = lax.dot_general(hamil, gbar, (((1,), (1,)), ((), ())), preferred_element_type=F32)
    return (d_green, d_chol, d_trial)


def nn(a, b):
    return jnp.dot(a, b, preferred_element_type=F32)


def nt(a, b):
    return lax.dot_general(a, b, (((1,), (1,)), ((), ())), preferred_element_type=F32)


def kernel_of(exch, cot):
    row = lax.broadcasted_iota(jnp.int32, exch.shape, 0)
    col = lax.broadcasted_iota(jnp.int32, exch.shape, 1)
    on_diagonal = jnp.where(row == col, exch, 0.0)
    coul = jnp.sum(jnp.sum(on_diagonal, axis=0, keepdims=True), axis=1, keepdims=True)
    return (cot * (jnp.where(row == col, coul, 0.0) - exch)).astype(BF16)


def row_groups(rows, width):
    fits = [n for n in range(1, rows + 1) if rows % n == 0 and rows // n % SUBLANES == 0]
    padded = {n: -(-n * width // LANES) * LANES / n for n in fits}
    least = min(padded.values())
    return min(n for n in fits if padded[n] <= 1.03 * least)


def half_of(half, kernels, cot, chol_ref, trial, hamil_ref, part_ref, packed_ref, groups):
    nocc, norb = chol_ref.shape[1:]
    width = norb // 4
    height = nocc // groups
    begin = half * 2 * width
    window = slice(begin // LANES * LANES, begin + 2 * width)
    total = cot * nn(trial, hamil_ref[:, window])
    for v, kernel in enumerate(kernels):
        total += nn(kernel, chol_ref[v, :, window])
    part_ref[:, : total.shape[1]] = total
    for q in range(2):
        left = begin - window.start + q * width
        for r in range(groups):
            packed_ref[q, :, r * width : (r + 1) * width] = part_ref[
                r * height : (r + 1) * height, left : left + width
            ]


def crossing_kernel(groups, *refs):
    cot_in, green_in, chol_in, trial_in, hamil_in = refs[:5]
    second_ref, third_ref, kernel_ref, green_ref, chol_ref, trial_ref, hamil_ref = refs[5:12]
    cot_ref, part_ref, packed_ref, sems = refs[12:]
    vectors = chol_ref.shape[0]
    copies = [pltpu.make_async_copy(green_in, green_ref, sems.at[0])]
    for v in range(vectors):
        copies.append(pltpu.make_async_copy(chol_in.at[v], chol_ref.at[v], sems.at[1 + v]))
    copies.append(pltpu.make_async_copy(trial_in, trial_ref, sems.at[1 + vectors]))
    copies.append(pltpu.make_async_copy(hamil_in, hamil_ref, sems.at[2 + vectors]))
    copies.append(pltpu.make_async_copy(cot_in, cot_ref, sems.at[3 + vectors]))
    for copy in copies[-1:] + copies[:-1]:
        copy.start()
    rank = lax.axis_index("chol")
    copies[-1].wait()
    cot = cot_ref[lax.axis_index("walk")]
    copies[0].wait()
    for v in range(vectors):
        copies[1 + v].wait()
        kernel_ref[v] = kernel_of(nt(chol_ref[v], green_ref[0]), cot)
    copies[1 + vectors].wait()
    copies[2 + vectors].wait()
    for half in range(2):

        @pl.when(rank // 2 != half)
        def _():
            kernels = [kernel_ref[v] for v in range(vectors)]
            trial = trial_ref[...].T
            half_of(half, kernels, cot, chol_ref, trial, hamil_ref, part_ref, packed_ref, groups)

    second_ref[...] = packed_ref[rank % 2].astype(BF16)
    third_ref[...] = packed_ref[1 - rank % 2].astype(BF16)


def staying_kernel(groups, *refs):
    cot_ref, kernel_ref, chol_ref, trial_ref, hamil_ref = refs[:5]
    first_ref, own_ref, part_ref, packed_ref = refs[5:]
    rank = lax.axis_index("chol")
    cot = cot_ref[lax.axis_index("walk")]
    for half in range(2):

        @pl.when(rank // 2 == half)
        def _():
            kernels = [kernel_ref[v] for v in range(chol_ref.shape[0])]
            trial = trial_ref[...].T
            half_of(half, kernels, cot, chol_ref, trial, hamil_ref, part_ref, packed_ref, groups)

    first_ref[...] = packed_ref[1 - rank % 2].astype(BF16)
    own_ref[...] = packed_ref[rank % 2]


def half_scratch(nocc, norb, block):
    wide = -(-(norb // 2) // LANES) * LANES + LANES
    return [pltpu.VMEM((nocc, wide), F32), pltpu.VMEM((2,) + block, F32)]


def shape_of(x):
    return jax.ShapeDtypeStruct(x.shape, x.dtype)


def crossing(groups, cot, green, chol, trial, hamil):
    _, nocc, norb = green.shape
    vectors = chol.shape[0]
    block = (nocc // groups, groups * (norb // 4))
    vmem = pl.BlockSpec(memory_space=pltpu.VMEM)
    loaded = (cot, green, chol, trial, hamil)
    loaded = [pltpu.with_memory_space_constraint(x, pltpu.HBM) for x in loaded]
    return pl.pallas_call(
        functools.partial(crossing_kernel, groups),
        out_shape=[jax.ShapeDtypeStruct(block, BF16)] * 2
        + [jax.ShapeDtypeStruct((vectors, nocc, nocc), BF16)]
        + [shape_of(x) for x in (green, chol, trial, hamil)],
        in_specs=[pl.BlockSpec(memory_space=pltpu.HBM)] * 5,
        out_specs=[vmem] * 7,
        scratch_shapes=[pltpu.SMEM(cot.shape, F32)]
        + half_scratch(nocc, norb, block)
        + [pltpu.SemaphoreType.DMA((4 + vectors,))],
        cost_estimate=pl.CostEstimate(
            flops=nocc * norb * (3 * vectors * nocc + trial.shape[0]),
            bytes_accessed=2 * (green.size + chol.size + trial.size + hamil.size),
            transcendentals=0,
        ),
        compiler_params=pltpu.CompilerParams(vmem_limit_bytes=16 * MIB),
        name="crossing",
    )(*loaded)


def staying(groups, cot, kernels, chol, trial, hamil):
    vectors, nocc, norb = chol.shape
    block = (nocc // groups, groups * (norb // 4))
    vmem = pl.BlockSpec(memory_space=pltpu.VMEM)
    return pl.pallas_call(
        functools.partial(staying_kernel, groups),
        out_shape=[jax.ShapeDtypeStruct(block, BF16), jax.ShapeDtypeStruct(block, F32)],
        in_specs=[pl.BlockSpec(memory_space=pltpu.SMEM)] + [vmem] * 4,
        out_specs=[vmem] * 2,
        scratch_shapes=half_scratch(nocc, norb, block),
        cost_estimate=pl.CostEstimate(
            flops=nocc * norb * (vectors * nocc + trial.shape[0]),
            bytes_accessed=2 * (chol.size + trial.size + hamil.size),
            transcendentals=0,
        ),
        compiler_params=pltpu.CompilerParams(vmem_limit_bytes=16 * MIB),
        name="staying",
    )(cot, kernels, chol, trial, hamil)


def walkers_kernel(order, old, last, ways, cot_ref, chol_ref, *refs):
    count = len(order)
    greens, refs = refs[:count], refs[count:]
    old_chol, old_bar = refs[:2] if old else (None, None)
    refs = refs[2 * old :]
    hamil_ref, refs = (refs[0], refs[1:]) if last else (None, refs)
    d_chol_ref, second_ref, share = refs
    rank = lax.axis_index("walk")
    width = share.shape[2]
    for place in range(ways):

        @pl.when(rank == place)
        def _():
            for n in range(count):
                share[n] = greens[n][0, :, place * width : (place + 1) * width]

    for v in range(chol_ref.shape[0]):
        total = old_chol[v] if old else 0.0
        for n in range(count):
            flipped = nt(greens[n][0], chol_ref[v])
            total += nn(kernel_of(flipped, cot_ref[rank ^ order[n]]), share[n])
        d_chol_ref[v] = total
    bar = old_bar[...] if old else 0.0
    for n in range(count):
        bar += cot_ref[rank ^ order[n]] * greens[n][0].astype(F32)
    if last:
        second_ref[...] = nt(hamil_ref[...], bar.astype(BF16))
    else:
        second_ref[...] = bar


def walkers(order, ways, cot, chol, greens, old=(), hamil=None):
    vectors, nocc, norb = chol.shape
    width = norb // ways
    last = hamil is not None
    rest = (*greens, *old) + ((hamil,) if last else ())
    vmem = pl.BlockSpec(memory_space=pltpu.VMEM)
    second = (hamil.shape[0], nocc) if last else (nocc, norb)
    return pl.pallas_call(
        functools.partial(walkers_kernel, order, bool(old), last, ways),
        out_shape=[
            jax.ShapeDtypeStruct((vectors, nocc, width), F32),
            jax.ShapeDtypeStruct(second, F32),
        ],
        in_specs=[pl.BlockSpec(memory_space=pltpu.SMEM)] + [vmem] * (1 + len(rest)),
        out_specs=[vmem] * 2,
        scratch_shapes=[pltpu.VMEM((len(order), nocc, width), BF16)],
        cost_estimate=pl.CostEstimate(
            flops=2 * nocc * nocc * vectors * len(order) * (norb + width)
            + (2 * hamil.size * nocc if last else 0),
            bytes_accessed=2 * (chol.size + len(order) * nocc * norb),
            transcendentals=0,
        ),
        compiler_params=pltpu.CompilerParams(vmem_limit_bytes=16 * MIB),
    )(cot, chol, *rest)


def joined_kernel(groups, own_ref, *refs):
    received, out_ref, sum_ref = refs[:-2], refs[-2], refs[-1]
    total = own_ref[...]
    for part in received:
        total += part[...].astype(F32)
    sum_ref[...] = total
    height = total.shape[0]
    width = total.shape[1] // groups
    for r in range(groups):
        out_ref[0, r * height : (r + 1) * height, :] = sum_ref[:, r * width : (r + 1) * width]


def joined(groups, own, received):
    height, long = own.shape
    vmem = pl.BlockSpec(memory_space=pltpu.VMEM)
    return pl.pallas_call(
        functools.partial(joined_kernel, groups),
        out_shape=jax.ShapeDtypeStruct((1, groups * height, long // groups), F32),
        in_specs=[vmem] * (1 + len(received)),
        out_specs=vmem,
        scratch_shapes=[pltpu.VMEM((height, long), F32)],
        cost_estimate=pl.CostEstimate(
            flops=own.size * 4, bytes_accessed=own.size * 16, transcendentals=0
        ),
        compiler_params=pltpu.CompilerParams(vmem_limit_bytes=16 * MIB),
        name="joined",
    )(own, *received)


def swapped(x, axis, bits):
    return lax.ppermute(x, axis, [(i, i ^ bits) for i in range(lax.axis_size(axis))])


def shards(green, chol, trial, hamil, energy_cot):
    ways = lax.axis_size("walk")
    _, nocc, norb = green.shape
    groups = row_groups(nocc, norb // lax.axis_size("chol"))
    far = swapped(green, "walk", 2)
    near = swapped(green, "walk", 1)
    second, third, kernels, green, chol, trial, hamil = crossing(
        groups, energy_cot, green, chol, trial, hamil
    )
    from_second = swapped(second, "chol", 2)
    from_third = swapped(third, "chol", 3)
    first, own = staying(groups, energy_cot, kernels, chol, trial, hamil)
    from_first = swapped(first, "chol", 1)
    sums = walkers((0, 1), ways, energy_cot, chol, [green, near])
    other = swapped(far, "walk", 1)
    sums = walkers((2,), ways, energy_cot, chol, [far], sums)
    d_chol, d_trial = walkers((3,), ways, energy_cot, chol, [other], sums, hamil)
    d_green = joined(groups, own, [from_first, from_second, from_third])
    return (d_green, d_chol, d_trial)


def solution(mesh):
    fits = mesh.shape["walk"] == 4 and mesh.shape["chol"] == 4

    def body(green, *rest):
        if fits and green.shape[0] == 1 and green.shape[1] % SUBLANES == 0:
            return shards(green, *rest)
        return plain(green, *rest)

    return jax.shard_map(
        body,
        mesh=mesh,
        in_specs=(
            P(("groups", "walk"), None, None),
            P(("groups", "chol"), None, None),
            P(("groups", "chol"), None),
            P("chol", None),
            P("groups"),
        ),
        out_specs=(
            P(("groups", "walk"), None, "chol"),
            P(("groups", "chol"), None, "walk"),
            P(("groups", "chol"), None),
        ),
        check_vma=False,
    )
```

```python
import functools

import jax
import jax.numpy as jnp
from jax import lax
from jax.experimental import pallas as pl
from jax.experimental.pallas import tpu as pltpu
from jax.sharding import PartitionSpec as P


F32 = jnp.float32
BF16 = jnp.bfloat16
LANES = 128
SUBLANES = 8
MIB = 1024 * 1024


def plain(green, chol, trial, hamil, energy_cot):
    walk_rank = lax.axis_index("walk")
    walk_rows = green.shape[0]
    cot_own = lax.dynamic_slice_in_dim(energy_cot, walk_rank * walk_rows, walk_rows, 0)
    hrot_part = lax.dot_general(
        trial, hamil, (((0,), (0,)), ((), ())), preferred_element_type=F32
    )
    identity = jnp.eye(trial.shape[1], dtype=F32)
    quarter = green.shape[2] // lax.axis_size("walk")
    greens = lax.all_gather(green, "walk", axis=0, tiled=True)
    coulomb = jnp.einsum("cip,wip->cw", chol, greens, preferred_element_type=F32)
    exchange_mat = jnp.einsum("cip,wjp->cwij", chol, greens, preferred_element_type=F32)
    kernel_mat = (
        energy_cot[None, :, None, None] * (coulomb[:, :, None, None] * identity - exchange_mat)
    ).astype(BF16)
    kernel_own = lax.dynamic_slice_in_dim(kernel_mat, walk_rank * walk_rows, walk_rows, 1)
    green_part = jnp.einsum("cwij,cjp->wip", kernel_own, chol, preferred_element_type=F32)
    green_part = green_part + cot_own[:, None, None] * hrot_part[None]
    d_green = lax.psum_scatter(green_part, "chol", scatter_dimension=2, tiled=True)
    green_share = lax.dynamic_slice_in_dim(greens, walk_rank * quarter, quarter, 2)
    d_chol = jnp.einsum("cwji,wjp->cip", kernel_mat, green_share, preferred_element_type=F32)
    gbar = jnp.einsum(
        "w,wip->ip",
        energy_cot,
        greens,
        precision=lax.Precision.HIGHEST,
        preferred_element_type=F32,
    ).astype(BF16)
    d_trial = lax.dot_general(hamil, gbar, (((1,), (1,)), ((), ())), preferred_element_type=F32)
    return (d_green, d_chol, d_trial)


def nn(a, b):
    return jnp.dot(a, b, preferred_element_type=F32)


def nt(a, b):
    return lax.dot_general(a, b, (((1,), (1,)), ((), ())), preferred_element_type=F32)


def kernel_of(exch, cot):
    row = lax.broadcasted_iota(jnp.int32, exch.shape, 0)
    col = lax.broadcasted_iota(jnp.int32, exch.shape, 1)
    on_diagonal = jnp.where(row == col, exch, 0.0)
    coul = jnp.sum(jnp.sum(on_diagonal, axis=0, keepdims=True), axis=1, keepdims=True)
    return (cot * jnp.where(row == col, coul - exch, -exch)).astype(BF16)


def row_groups(rows, width):
    fits = [n for n in range(1, rows + 1) if rows % n == 0 and rows // n % SUBLANES == 0]
    padded = {n: -(-n * width // LANES) * LANES / n for n in fits}
    least = min(padded.values())
    return min(n for n in fits if padded[n] <= 1.03 * least)


def half_of(half, kernel_ref, cot, chol_ref, trial_ref, hamil_ref, part_ref, packed_ref, groups):
    nocc, norb = chol_ref.shape[1:]
    width = norb // 4
    height = nocc // groups
    skew = 2 * width % LANES
    size = 2 * width + skew
    window = pl.ds(pl.multiple_of(half * (2 * width - skew), LANES), size)
    total = cot * nn(trial_ref[...].T, hamil_ref[:, window])
    for v in range(chol_ref.shape[0]):
        total += nn(kernel_ref[v], chol_ref[v, :, window])
    part_ref[:, :size] = total
    for place in range(2):

        @pl.when(half == place)
        def _():
            for q in range(2):
                left = place * skew + q * width
                for r in range(groups):
                    packed_ref[q, :, r * width : (r + 1) * width] = part_ref[
                        r * height : (r + 1) * height, left : left + width
                    ]


def crossing_kernel(groups, *refs):
    _, green_ref, chol_ref, cot_in, trial_in, hamil_in = refs[:6]
    second_ref, third_ref, kept_ref, paired_ref, kernel_ref, trial_ref, hamil_ref = refs[6:13]
    cot_ref, part_ref, packed_ref, sems = refs[13:]
    cut = second_ref.shape[0]
    cot_copy = pltpu.make_async_copy(cot_in, cot_ref, sems.at[0])
    trial_copy = pltpu.make_async_copy(trial_in, trial_ref, sems.at[1])
    hamil_copy = pltpu.make_async_copy(hamil_in, hamil_ref, sems.at[2])
    cot_copy.start()
    trial_copy.start()
    hamil_copy.start()
    vectors = chol_ref.shape[0]
    rank = lax.axis_index("chol")
    exchange = [nt(chol_ref[v], green_ref[0]) for v in range(vectors)]
    cot_copy.wait()
    cot = cot_ref[lax.axis_index("walk")]
    for v in range(vectors):
        kernel_ref[v] = kernel_of(exchange[v], cot)
    trial_copy.wait()
    hamil_copy.wait()
    half_of(
        1 - rank // 2, kernel_ref, cot, chol_ref, trial_ref, hamil_ref, part_ref, packed_ref, groups
    )
    second_ref[...] = packed_ref[rank % 2, :cut].astype(BF16)
    third_ref[...] = packed_ref[1 - rank % 2, :cut].astype(BF16)
    kept_ref[...] = packed_ref[rank % 2, cut:]
    paired_ref[...] = packed_ref[1 - rank % 2, cut:].astype(BF16)


def staying_kernel(groups, *refs):
    cot_ref, kernel_ref, chol_ref, trial_ref, hamil_ref = refs[:5]
    first_ref, own_ref, part_ref, packed_ref = refs[5:]
    rank = lax.axis_index("chol")
    cot = cot_ref[lax.axis_index("walk")]
    half_of(
        rank // 2, kernel_ref, cot, chol_ref, trial_ref, hamil_ref, part_ref, packed_ref, groups
    )
    first_ref[...] = packed_ref[1 - rank % 2].astype(BF16)
    own_ref[...] = packed_ref[rank % 2]


def half_scratch(nocc, norb, block):
    wide = -(-(norb // 2) // LANES) * LANES + LANES
    return [pltpu.VMEM((nocc, wide), F32), pltpu.VMEM((2,) + block, F32)]


def shape_of(x):
    return jax.ShapeDtypeStruct(x.shape, x.dtype)


def opening_kernel(out_ref):
    out_ref[...] = jnp.zeros_like(out_ref)


def opening():
    return pl.pallas_call(
        opening_kernel,
        out_shape=jax.ShapeDtypeStruct((SUBLANES, LANES), F32),
        out_specs=pl.BlockSpec(memory_space=pltpu.VMEM),
        cost_estimate=pl.CostEstimate(flops=4 * 10**9, bytes_accessed=4096, transcendentals=0),
        compiler_params=pltpu.CompilerParams(vmem_limit_bytes=MIB, has_side_effects=True),
        name="opening",
    )()


def crossing(groups, cut, token, cot, green, chol, trial, hamil):
    _, nocc, norb = green.shape
    vectors = chol.shape[0]
    block = (nocc // groups, groups * (norb // 4))
    rest = (block[0] - cut, block[1])
    vmem = pl.BlockSpec(memory_space=pltpu.VMEM)
    loaded = [pltpu.with_memory_space_constraint(x, pltpu.HBM) for x in (cot, trial, hamil)]
    return pl.pallas_call(
        functools.partial(crossing_kernel, groups),
        out_shape=[jax.ShapeDtypeStruct((cut, block[1]), BF16)] * 2
        + [jax.ShapeDtypeStruct(rest, F32), jax.ShapeDtypeStruct(rest, BF16)]
        + [jax.ShapeDtypeStruct((vectors, nocc, nocc), BF16), shape_of(trial), shape_of(hamil)],
        in_specs=[vmem] * 3 + [pl.BlockSpec(memory_space=pltpu.HBM)] * 3,
        out_specs=[vmem] * 7,
        scratch_shapes=[pltpu.SMEM(cot.shape, F32)]
        + half_scratch(nocc, norb, block)
        + [pltpu.SemaphoreType.DMA((3,))],
        cost_estimate=pl.CostEstimate(
            flops=nocc * norb * (3 * vectors * nocc + trial.shape[0]),
            bytes_accessed=2 * (green.size + chol.size + trial.size + hamil.size),
            transcendentals=0,
        ),
        compiler_params=pltpu.CompilerParams(vmem_limit_bytes=16 * MIB),
        name="crossing",
    )(token, green, chol, *loaded)


def staying(groups, cot, kernels, chol, trial, hamil):
    vectors, nocc, norb = chol.shape
    block = (nocc // groups, groups * (norb // 4))
    vmem = pl.BlockSpec(memory_space=pltpu.VMEM)
    return pl.pallas_call(
        functools.partial(staying_kernel, groups),
        out_shape=[jax.ShapeDtypeStruct(block, BF16), jax.ShapeDtypeStruct(block, F32)],
        in_specs=[pl.BlockSpec(memory_space=pltpu.SMEM)] + [vmem] * 4,
        out_specs=[vmem] * 2,
        scratch_shapes=half_scratch(nocc, norb, block),
        cost_estimate=pl.CostEstimate(
            flops=nocc * norb * (vectors * nocc + trial.shape[0]),
            bytes_accessed=2 * (chol.size + trial.size + hamil.size),
            transcendentals=0,
        ),
        compiler_params=pltpu.CompilerParams(vmem_limit_bytes=16 * MIB),
        name="staying",
    )(cot, kernels, chol, trial, hamil)


def unpacked_rows(out_ref, packed_ref, groups):
    height, width = packed_ref.shape[0], packed_ref.shape[1] // groups
    for r in range(groups):
        out_ref[r * height : (r + 1) * height, :] = packed_ref[:, r * width : (r + 1) * width]


def share_of(rank, norb, ways):
    width = norb // ways
    offsets = [w * width % LANES for w in range(ways)]
    begin = rank * width // LANES * LANES
    return pl.ds(pl.multiple_of(begin, LANES), width + max(offsets)), rank * width - begin


def window_size(norb, ways):
    width = norb // ways
    return width + max(w * width % LANES for w in range(ways))


def call(kernel, out_shape, args, flops, moved, **more):
    vmem = pl.BlockSpec(memory_space=pltpu.VMEM)
    smem = pl.BlockSpec(memory_space=pltpu.SMEM)
    return pl.pallas_call(
        kernel,
        out_shape=out_shape,
        in_specs=[smem if x.ndim == 1 else vmem for x in args],
        cost_estimate=pl.CostEstimate(flops=flops, bytes_accessed=moved, transcendentals=0),
        compiler_params=pltpu.CompilerParams(vmem_limit_bytes=16 * MIB),
        **{"out_specs": [vmem] * len(out_shape), **more},
    )(*args)


def pair_kernel(kept_ref, received_ref, out_ref):
    out_ref[...] = (kept_ref[...] + received_ref[...].astype(F32)).astype(BF16)


def pair_sum(kept, received):
    out = [shape_of(received)]
    return call(pair_kernel, out, (kept, received), kept.size, 8 * kept.size)[0]


def early_kernel(ways, cot_ref, chol_ref, hamil_ref, green_ref, near_ref, kernel_ref, *outs):
    d_chol_ref, d_trial_ref = outs
    rank = lax.axis_index("walk")
    vectors, _, norb = chol_ref.shape
    window, _ = share_of(rank, norb, ways)
    flipped = [nt(near_ref[0], chol_ref[v]) for v in range(chol_ref.shape[0])]
    total = cot_ref[rank] * nt(hamil_ref[...], green_ref[0])
    d_trial_ref[...] = total + cot_ref[rank ^ 1] * nt(hamil_ref[...], near_ref[0])
    for v in range(vectors):
        own = nn(kernel_ref[v].T, green_ref[0, :, window])
        near = kernel_of(flipped[v], cot_ref[rank ^ 1])
        d_chol_ref[v] = own + nn(near, near_ref[0, :, window])


def middle_kernel(bits, ways, cot_ref, chol_ref, hamil_ref, green_ref, *refs):
    old_chol, old_trial, d_chol_ref, d_trial_ref = refs
    rank = lax.axis_index("walk")
    cot = cot_ref[rank ^ bits]
    vectors, _, norb = chol_ref.shape
    window, _ = share_of(rank, norb, ways)
    flipped = [nt(green_ref[0], chol_ref[v]) for v in range(chol_ref.shape[0])]
    d_trial_ref[...] = old_trial[...] + cot * nt(hamil_ref[...], green_ref[0])
    for v in range(vectors):
        kernel = kernel_of(flipped[v], cot)
        d_chol_ref[v] = old_chol[v] + nn(kernel, green_ref[0, :, window])


def walkers(kernel, ways, cot, chol, hamil, greens, *rest):
    vectors, nocc, norb = chol.shape
    size = window_size(norb, ways)
    return call(
        kernel,
        [
            jax.ShapeDtypeStruct((vectors, nocc, size), F32),
            jax.ShapeDtypeStruct((hamil.shape[0], nocc), F32),
        ],
        (cot, chol, hamil, *greens, *rest),
        2 * nocc * len(greens) * (nocc * vectors * (norb + size) + hamil.size),
        2 * (chol.size + len(greens) * nocc * norb),
    )


def late_kernel(bits, ways, cot_ref, chol_ref, hamil_ref, green_ref, *refs):
    old_chol, old_trial, d_chol_ref, d_trial_ref, wide_ref = refs
    rank = lax.axis_index("walk")
    cot = cot_ref[rank ^ bits]
    vectors, _, norb = chol_ref.shape
    window, offset = share_of(rank, norb, ways)
    flipped = [nt(green_ref[0], chol_ref[v]) for v in range(vectors)]
    d_trial_ref[...] = old_trial[...] + cot * nt(hamil_ref[...], green_ref[0])
    for v in range(vectors):
        kernel = kernel_of(flipped[v], cot)
        total = old_chol[v] + nn(kernel, green_ref[0, :, window])
        wide_ref[v, :, : total.shape[1]] = total
        moved = pltpu.roll(wide_ref[v], wide_ref.shape[2] - offset, 1)
        d_chol_ref[v] = moved[:, : norb // ways]


def late(bits, ways, cot, chol, hamil, green, old):
    vectors, nocc, norb = chol.shape
    wide = -(-window_size(norb, ways) // LANES) * LANES
    shapes = [(vectors, nocc, norb // ways), (hamil.shape[0], nocc)]
    return call(
        functools.partial(late_kernel, bits, ways),
        [jax.ShapeDtypeStruct(shape, F32) for shape in shapes],
        (cot, chol, hamil, green, *old),
        2 * nocc * (nocc * vectors * (norb + wide) + hamil.size),
        2 * (chol.size + hamil.size + nocc * norb),
        scratch_shapes=[pltpu.VMEM((vectors, nocc, wide), F32)],
    )


def joined_kernel(groups, cut, chol_ref, trial_ref, *refs):
    own_ref, first_ref, second_ref, third_ref, pair_ref = refs[:5]
    green_out, chol_out, trial_out, sum_ref, d_green, sems = refs[5:]
    copies = [
        pltpu.make_async_copy(trial_ref, trial_out, sems.at[1]),
        pltpu.make_async_copy(chol_ref, chol_out, sems.at[2]),
    ]
    for copy in copies:
        copy.start()
    total = own_ref[...] + first_ref[...].astype(F32)
    sum_ref[:cut] = total[:cut] + second_ref[...].astype(F32) + third_ref[...].astype(F32)
    sum_ref[cut:] = total[cut:] + pair_ref[...].astype(F32)
    unpacked_rows(d_green.at[0], sum_ref, groups)
    copies.append(pltpu.make_async_copy(d_green, green_out, sems.at[0]))
    copies[-1].start()
    for copy in copies:
        copy.wait()


def joined(groups, cut, d_chol, d_trial, own, received):
    height, long = own.shape
    shape = (1, groups * height, long // groups)
    return call(
        functools.partial(joined_kernel, groups, cut),
        [jax.ShapeDtypeStruct(shape, F32), shape_of(d_chol), shape_of(d_trial)],
        (d_chol, d_trial, own, *received),
        own.size * 4,
        own.size * 16,
        out_specs=[pl.BlockSpec(memory_space=pltpu.HBM)] * 3,
        scratch_shapes=[
            pltpu.VMEM((height, long), F32),
            pltpu.VMEM(shape, F32),
            pltpu.SemaphoreType.DMA((3,)),
        ],
    )


def swapped(x, axis, bits):
    return lax.ppermute(x, axis, [(i, i ^ bits) for i in range(lax.axis_size(axis))])


def shards(green, chol, trial, hamil, energy_cot):
    ways = lax.axis_size("walk")
    _, nocc, norb = green.shape
    groups = row_groups(nocc, norb // lax.axis_size("chol"))
    cut = nocc // groups * 2 // 5 // SUBLANES * SUBLANES
    far = swapped(green, "walk", 2)
    token = opening()
    second, third, kept, paired, kernels, trial, hamil = crossing(
        groups, cut, token, energy_cot, green, chol, trial, hamil
    )
    paired = swapped(paired, "chol", 1)
    second = swapped(second, "chol", 2)
    third = swapped(third, "chol", 3)
    near = swapped(green, "walk", 1)
    both = swapped(pair_sum(kept, paired), "chol", 2)
    first, own = staying(groups, energy_cot, kernels, chol, trial, hamil)
    first = swapped(first, "chol", 1)
    early = functools.partial(early_kernel, ways)
    same = (ways, energy_cot, chol, hamil)
    sums = walkers(early, *same, [green, near], kernels)
    other = swapped(far, "walk", 1)
    middle = functools.partial(middle_kernel, 2, ways)
    sums = walkers(middle, *same, [far], *sums)
    sums = late(3, *same, other, sums)
    return tuple(joined(groups, cut, *sums, own, (first, second, third, both)))


def solution(mesh):
    fits = mesh.shape["walk"] == 4 and mesh.shape["chol"] == 4

    def body(green, *rest):
        if fits and green.shape[0] == 1 and green.shape[1] % SUBLANES == 0:
            return shards(green, *rest)
        return plain(green, *rest)

    return jax.shard_map(
        body,
        mesh=mesh,
        in_specs=(
            P(("groups", "walk"), None, None),
            P(("groups", "chol"), None, None),
            P(("groups", "chol"), None),
            P("chol", None),
            P("groups"),
        ),
        out_specs=(
            P(("groups", "walk"), None, "chol"),
            P(("groups", "chol"), None, "walk"),
            P(("groups", "chol"), None),
        ),
        check_vma=False,
    )
```

```python
import functools

import jax
import jax.numpy as jnp
from jax import lax
from jax.experimental import pallas as pl
from jax.experimental.pallas import tpu as pltpu
from jax.sharding import PartitionSpec as P


F32 = jnp.float32
BF16 = jnp.bfloat16
LANES = 128
SUBLANES = 8
MIB = 1024 * 1024


def plain(green, chol, trial, hamil, energy_cot):
    walk_rank = lax.axis_index("walk")
    walk_rows = green.shape[0]
    cot_own = lax.dynamic_slice_in_dim(energy_cot, walk_rank * walk_rows, walk_rows, 0)
    hrot_part = lax.dot_general(
        trial, hamil, (((0,), (0,)), ((), ())), preferred_element_type=F32
    )
    identity = jnp.eye(trial.shape[1], dtype=F32)
    quarter = green.shape[2] // lax.axis_size("walk")
    greens = lax.all_gather(green, "walk", axis=0, tiled=True)
    coulomb = jnp.einsum("cip,wip->cw", chol, greens, preferred_element_type=F32)
    exchange_mat = jnp.einsum("cip,wjp->cwij", chol, greens, preferred_element_type=F32)
    kernel_mat = (
        energy_cot[None, :, None, None] * (coulomb[:, :, None, None] * identity - exchange_mat)
    ).astype(BF16)
    kernel_own = lax.dynamic_slice_in_dim(kernel_mat, walk_rank * walk_rows, walk_rows, 1)
    green_part = jnp.einsum("cwij,cjp->wip", kernel_own, chol, preferred_element_type=F32)
    green_part = green_part + cot_own[:, None, None] * hrot_part[None]
    d_green = lax.psum_scatter(green_part, "chol", scatter_dimension=2, tiled=True)
    green_share = lax.dynamic_slice_in_dim(greens, walk_rank * quarter, quarter, 2)
    d_chol = jnp.einsum("cwji,wjp->cip", kernel_mat, green_share, preferred_element_type=F32)
    gbar = jnp.einsum(
        "w,wip->ip",
        energy_cot,
        greens,
        precision=lax.Precision.HIGHEST,
        preferred_element_type=F32,
    ).astype(BF16)
    d_trial = lax.dot_general(hamil, gbar, (((1,), (1,)), ((), ())), preferred_element_type=F32)
    return (d_green, d_chol, d_trial)


def nn(a, b):
    return jnp.dot(a, b, preferred_element_type=F32)


def nt(a, b):
    return lax.dot_general(a, b, (((1,), (1,)), ((), ())), preferred_element_type=F32)


def kernel_of(exch, cot):
    row = lax.broadcasted_iota(jnp.int32, exch.shape, 0)
    col = lax.broadcasted_iota(jnp.int32, exch.shape, 1)
    on_diagonal = jnp.where(row == col, exch, 0.0)
    coul = jnp.sum(jnp.sum(on_diagonal, axis=0, keepdims=True), axis=1, keepdims=True)
    return (cot * jnp.where(row == col, coul - exch, -exch)).astype(BF16)


def row_groups(rows, width):
    fits = [n for n in range(1, rows + 1) if rows % n == 0 and rows // n % SUBLANES == 0]
    padded = {n: -(-n * width // LANES) * LANES / n for n in fits}
    least = min(padded.values())
    return min(n for n in fits if padded[n] <= 1.03 * least)


def half_of(half, kernel_ref, cot, chol_ref, trial_ref, hamil_ref, part_ref, packed_ref, groups):
    nocc, norb = chol_ref.shape[1:]
    width = norb // 4
    height = nocc // groups
    skew = 2 * width % LANES
    size = 2 * width + skew
    window = pl.ds(pl.multiple_of(half * (2 * width - skew), LANES), size)
    total = cot * nn(trial_ref[...].T, hamil_ref[:, window])
    for v in range(chol_ref.shape[0]):
        total += nn(kernel_ref[v], chol_ref[v, :, window])
    part_ref[:, :size] = total
    for place in range(2):

        @pl.when(half == place)
        def _():
            for q in range(2):
                left = place * skew + q * width
                for r in range(groups):
                    packed_ref[q, :, r * width : (r + 1) * width] = part_ref[
                        r * height : (r + 1) * height, left : left + width
                    ]


def crossing_kernel(groups, *refs):
    _, green_ref, chol_ref, cot_in, trial_in, hamil_in = refs[:6]
    second_ref, third_ref, kept_ref, paired_ref, kernel_ref, trial_ref, hamil_ref = refs[6:13]
    cot_ref, part_ref, packed_ref, sems = refs[13:]
    cut = second_ref.shape[0]
    cot_copy = pltpu.make_async_copy(cot_in, cot_ref, sems.at[0])
    trial_copy = pltpu.make_async_copy(trial_in, trial_ref, sems.at[1])
    hamil_copy = pltpu.make_async_copy(hamil_in, hamil_ref, sems.at[2])
    cot_copy.start()
    trial_copy.start()
    hamil_copy.start()
    vectors = chol_ref.shape[0]
    rank = lax.axis_index("chol")
    exchange = [nt(chol_ref[v], green_ref[0]) for v in range(vectors)]
    cot_copy.wait()
    cot = cot_ref[lax.axis_index("walk")]
    for v in range(vectors):
        kernel_ref[v] = kernel_of(exchange[v], cot)
    trial_copy.wait()
    hamil_copy.wait()
    half_of(
        1 - rank // 2, kernel_ref, cot, chol_ref, trial_ref, hamil_ref, part_ref, packed_ref, groups
    )
    second_ref[...] = packed_ref[rank % 2, :cut].astype(BF16)
    third_ref[...] = packed_ref[1 - rank % 2, :cut].astype(BF16)
    kept_ref[...] = packed_ref[rank % 2, cut:]
    paired_ref[...] = packed_ref[1 - rank % 2, cut:].astype(BF16)


def staying_kernel(groups, *refs):
    cot_ref, kernel_ref, chol_ref, trial_ref, hamil_ref = refs[:5]
    first_ref, own_ref, part_ref, packed_ref = refs[5:]
    rank = lax.axis_index("chol")
    cot = cot_ref[lax.axis_index("walk")]
    half_of(
        rank // 2, kernel_ref, cot, chol_ref, trial_ref, hamil_ref, part_ref, packed_ref, groups
    )
    first_ref[...] = packed_ref[1 - rank % 2].astype(BF16)
    own_ref[...] = packed_ref[rank % 2]


def half_scratch(nocc, norb, block):
    wide = -(-(norb // 2) // LANES) * LANES + LANES
    return [pltpu.VMEM((nocc, wide), F32), pltpu.VMEM((2,) + block, F32)]


def shape_of(x):
    return jax.ShapeDtypeStruct(x.shape, x.dtype)


def opening_kernel(out_ref):
    out_ref[...] = jnp.zeros_like(out_ref)


def opening():
    return pl.pallas_call(
        opening_kernel,
        out_shape=jax.ShapeDtypeStruct((SUBLANES, LANES), F32),
        out_specs=pl.BlockSpec(memory_space=pltpu.VMEM),
        cost_estimate=pl.CostEstimate(flops=4 * 10**9, bytes_accessed=4096, transcendentals=0),
        compiler_params=pltpu.CompilerParams(vmem_limit_bytes=MIB, has_side_effects=True),
        name="opening",
    )()


def crossing(groups, cut, token, cot, green, chol, trial, hamil):
    _, nocc, norb = green.shape
    vectors = chol.shape[0]
    block = (nocc // groups, groups * (norb // 4))
    rest = (block[0] - cut, block[1])
    vmem = pl.BlockSpec(memory_space=pltpu.VMEM)
    loaded = [pltpu.with_memory_space_constraint(x, pltpu.HBM) for x in (cot, trial, hamil)]
    return pl.pallas_call(
        functools.partial(crossing_kernel, groups),
        out_shape=[jax.ShapeDtypeStruct((cut, block[1]), BF16)] * 2
        + [jax.ShapeDtypeStruct(rest, F32), jax.ShapeDtypeStruct(rest, BF16)]
        + [jax.ShapeDtypeStruct((vectors, nocc, nocc), BF16), shape_of(trial), shape_of(hamil)],
        in_specs=[vmem] * 3 + [pl.BlockSpec(memory_space=pltpu.HBM)] * 3,
        out_specs=[vmem] * 7,
        scratch_shapes=[pltpu.SMEM(cot.shape, F32)]
        + half_scratch(nocc, norb, block)
        + [pltpu.SemaphoreType.DMA((3,))],
        cost_estimate=pl.CostEstimate(
            flops=nocc * norb * (3 * vectors * nocc + trial.shape[0]),
            bytes_accessed=2 * (green.size + chol.size + trial.size + hamil.size),
            transcendentals=0,
        ),
        compiler_params=pltpu.CompilerParams(vmem_limit_bytes=16 * MIB),
        name="crossing",
    )(token, green, chol, *loaded)


def staying(groups, cot, kernels, chol, trial, hamil):
    vectors, nocc, norb = chol.shape
    block = (nocc // groups, groups * (norb // 4))
    vmem = pl.BlockSpec(memory_space=pltpu.VMEM)
    return pl.pallas_call(
        functools.partial(staying_kernel, groups),
        out_shape=[jax.ShapeDtypeStruct(block, BF16), jax.ShapeDtypeStruct(block, F32)],
        in_specs=[pl.BlockSpec(memory_space=pltpu.SMEM)] + [vmem] * 4,
        out_specs=[vmem] * 2,
        scratch_shapes=half_scratch(nocc, norb, block),
        cost_estimate=pl.CostEstimate(
            flops=nocc * norb * (vectors * nocc + trial.shape[0]),
            bytes_accessed=2 * (chol.size + trial.size + hamil.size),
            transcendentals=0,
        ),
        compiler_params=pltpu.CompilerParams(vmem_limit_bytes=16 * MIB),
        name="staying",
    )(cot, kernels, chol, trial, hamil)


def unpacked_rows(out_ref, packed_ref, groups):
    height, width = packed_ref.shape[0], packed_ref.shape[1] // groups
    for r in range(groups):
        out_ref[r * height : (r + 1) * height, :] = packed_ref[:, r * width : (r + 1) * width]


def share_of(green_ref, wide_ref, rank, ways):
    norb = green_ref.shape[2]
    width = norb // ways
    begin = rank * width // LANES * LANES
    size = window_size(norb, ways)
    window = pl.ds(pl.multiple_of(begin, LANES), size)
    wide_ref[:, :size] = green_ref[0, :, window].astype(F32)
    moved = pltpu.roll(wide_ref[...], wide_ref.shape[1] - (rank * width - begin), 1)
    return moved[:, :width].astype(BF16)


def window_size(norb, ways):
    width = norb // ways
    return width + max(w * width % LANES for w in range(ways))


def window_scratch(nocc, norb, ways):
    return pltpu.VMEM((nocc, -(-window_size(norb, ways) // LANES) * LANES), F32)


def call(kernel, out_shape, args, flops, moved, **more):
    vmem = pl.BlockSpec(memory_space=pltpu.VMEM)
    smem = pl.BlockSpec(memory_space=pltpu.SMEM)
    return pl.pallas_call(
        kernel,
        out_shape=out_shape,
        in_specs=[smem if x.ndim == 1 else vmem for x in args],
        cost_estimate=pl.CostEstimate(flops=flops, bytes_accessed=moved, transcendentals=0),
        compiler_params=pltpu.CompilerParams(vmem_limit_bytes=16 * MIB),
        **{"out_specs": [vmem] * len(out_shape), **more},
    )(*args)


def pair_kernel(kept_ref, received_ref, out_ref):
    out_ref[...] = (kept_ref[...] + received_ref[...].astype(F32)).astype(BF16)


def pair_sum(kept, received):
    out = [shape_of(received)]
    return call(pair_kernel, out, (kept, received), kept.size, 8 * kept.size)[0]


def early_kernel(ways, cot_ref, chol_ref, hamil_ref, green_ref, near_ref, kernel_ref, *refs):
    d_chol_ref, d_trial_ref, own_ref, near_wide = refs
    rank = lax.axis_index("walk")
    vectors = range(chol_ref.shape[0])
    flipped = [nt(near_ref[0], chol_ref[v]) for v in vectors]
    own_share = share_of(green_ref, own_ref, rank, ways)
    near_share = share_of(near_ref, near_wide, rank, ways)
    total = cot_ref[rank] * nt(hamil_ref[...], green_ref[0])
    d_trial_ref[...] = total + cot_ref[rank ^ 1] * nt(hamil_ref[...], near_ref[0])
    for v in vectors:
        own = nn(kernel_ref[v].T, own_share)
        near = kernel_of(flipped[v], cot_ref[rank ^ 1])
        d_chol_ref[v] = own + nn(near, near_share)


def walker_kernel(bits, ways, cot_ref, chol_ref, hamil_ref, green_ref, *refs):
    old_chol, old_trial, d_chol_ref, d_trial_ref, wide_ref = refs
    rank = lax.axis_index("walk")
    cot = cot_ref[rank ^ bits]
    vectors = range(chol_ref.shape[0])
    flipped = [nt(green_ref[0], chol_ref[v]) for v in vectors]
    share = share_of(green_ref, wide_ref, rank, ways)
    d_trial_ref[...] = old_trial[...] + cot * nt(hamil_ref[...], green_ref[0])
    for v in vectors:
        d_chol_ref[v] = old_chol[v] + nn(kernel_of(flipped[v], cot), share)


def walkers(kernel, ways, cot, chol, hamil, greens, *rest):
    vectors, nocc, norb = chol.shape
    width = norb // ways
    trial = jax.ShapeDtypeStruct((hamil.shape[0], nocc), F32)
    return call(
        kernel,
        [jax.ShapeDtypeStruct((vectors, nocc, width), F32), trial],
        (cot, chol, hamil, *greens, *rest),
        2 * nocc * len(greens) * (nocc * vectors * (norb + width) + hamil.size),
        2 * (chol.size + len(greens) * nocc * norb),
        scratch_shapes=[window_scratch(nocc, norb, ways)] * len(greens),
    )


def joined_kernel(groups, cut, chol_ref, trial_ref, *refs):
    own_ref, first_ref, second_ref, third_ref, pair_ref = refs[:5]
    green_out, chol_out, trial_out, sum_ref, d_green, sems = refs[5:]
    chol_copy = pltpu.make_async_copy(chol_ref, chol_out, sems.at[1])
    chol_copy.start()
    trial_copy = pltpu.make_async_copy(trial_ref, trial_out, sems.at[2])
    trial_copy.start()
    total = own_ref[...] + first_ref[...].astype(F32)
    sum_ref[:cut] = total[:cut] + second_ref[...].astype(F32) + third_ref[...].astype(F32)
    sum_ref[cut:] = total[cut:] + pair_ref[...].astype(F32)
    unpacked_rows(d_green.at[0], sum_ref, groups)
    green_copy = pltpu.make_async_copy(d_green, green_out, sems.at[0])
    green_copy.start()
    chol_copy.wait()
    trial_copy.wait()
    green_copy.wait()


def joined(groups, cut, d_chol, d_trial, own, received):
    height, long = own.shape
    shape = (1, groups * height, long // groups)
    return call(
        functools.partial(joined_kernel, groups, cut),
        [jax.ShapeDtypeStruct(shape, F32), shape_of(d_chol), shape_of(d_trial)],
        (d_chol, d_trial, own, *received),
        own.size * 4,
        own.size * 16,
        out_specs=[pl.BlockSpec(memory_space=pltpu.HBM)] * 3,
        scratch_shapes=[
            pltpu.VMEM((height, long), F32),
            pltpu.VMEM(shape, F32),
            pltpu.SemaphoreType.DMA((3,)),
        ],
    )


def swapped(x, axis, bits):
    return lax.ppermute(x, axis, [(i, i ^ bits) for i in range(lax.axis_size(axis))])


def shards(green, chol, trial, hamil, energy_cot):
    ways = lax.axis_size("walk")
    _, nocc, norb = green.shape
    groups = row_groups(nocc, norb // lax.axis_size("chol"))
    cut = nocc // groups * 2 // 5 // SUBLANES * SUBLANES
    far = swapped(green, "walk", 2)
    token = opening()
    second, third, kept, paired, kernels, trial, hamil = crossing(
        groups, cut, token, energy_cot, green, chol, trial, hamil
    )
    paired = swapped(paired, "chol", 1)
    second = swapped(second, "chol", 2)
    third = swapped(third, "chol", 3)
    near = swapped(green, "walk", 1)
    both = swapped(pair_sum(kept, paired), "chol", 2)
    first, own = staying(groups, energy_cot, kernels, chol, trial, hamil)
    first = swapped(first, "chol", 1)
    early = functools.partial(early_kernel, ways)
    same = (ways, energy_cot, chol, hamil)
    sums = walkers(early, *same, [green, near], kernels)
    other = swapped(far, "walk", 1)
    middle = functools.partial(walker_kernel, 2, ways)
    sums = walkers(middle, *same, [far], *sums)
    late = functools.partial(walker_kernel, 3, ways)
    sums = walkers(late, *same, [other], *sums)
    return tuple(joined(groups, cut, *sums, own, (first, second, third, both)))


def solution(mesh):
    fits = mesh.shape["walk"] == 4 and mesh.shape["chol"] == 4

    def body(green, *rest):
        if fits and green.shape[0] == 1 and green.shape[1] % SUBLANES == 0:
            return shards(green, *rest)
        return plain(green, *rest)

    return jax.shard_map(
        body,
        mesh=mesh,
        in_specs=(
            P(("groups", "walk"), None, None),
            P(("groups", "chol"), None, None),
            P(("groups", "chol"), None),
            P("chol", None),
            P("groups"),
        ),
        out_specs=(
            P(("groups", "walk"), None, "chol"),
            P(("groups", "chol"), None, "walk"),
            P(("groups", "chol"), None),
        ),
        check_vma=False,
    )
```

```python
import functools

import jax
import jax.numpy as jnp
from jax import lax
from jax.experimental import pallas as pl
from jax.experimental.pallas import tpu as pltpu
from jax.sharding import PartitionSpec as P


F32 = jnp.float32
BF16 = jnp.bfloat16
LANES = 128
SUBLANES = 8
MIB = 1024 * 1024


def plain(green, chol, trial, hamil, energy_cot):
    walk_rank = lax.axis_index("walk")
    walk_rows = green.shape[0]
    cot_own = lax.dynamic_slice_in_dim(energy_cot, walk_rank * walk_rows, walk_rows, 0)
    hrot_part = lax.dot_general(
        trial, hamil, (((0,), (0,)), ((), ())), preferred_element_type=F32
    )
    identity = jnp.eye(trial.shape[1], dtype=F32)
    quarter = green.shape[2] // lax.axis_size("walk")
    greens = lax.all_gather(green, "walk", axis=0, tiled=True)
    coulomb = jnp.einsum("cip,wip->cw", chol, greens, preferred_element_type=F32)
    exchange_mat = jnp.einsum("cip,wjp->cwij", chol, greens, preferred_element_type=F32)
    kernel_mat = (
        energy_cot[None, :, None, None] * (coulomb[:, :, None, None] * identity - exchange_mat)
    ).astype(BF16)
    kernel_own = lax.dynamic_slice_in_dim(kernel_mat, walk_rank * walk_rows, walk_rows, 1)
    green_part = jnp.einsum("cwij,cjp->wip", kernel_own, chol, preferred_element_type=F32)
    green_part = green_part + cot_own[:, None, None] * hrot_part[None]
    d_green = lax.psum_scatter(green_part, "chol", scatter_dimension=2, tiled=True)
    green_share = lax.dynamic_slice_in_dim(greens, walk_rank * quarter, quarter, 2)
    d_chol = jnp.einsum("cwji,wjp->cip", kernel_mat, green_share, preferred_element_type=F32)
    gbar = jnp.einsum(
        "w,wip->ip",
        energy_cot,
        greens,
        precision=lax.Precision.HIGHEST,
        preferred_element_type=F32,
    ).astype(BF16)
    d_trial = lax.dot_general(hamil, gbar, (((1,), (1,)), ((), ())), preferred_element_type=F32)
    return (d_green, d_chol, d_trial)


def nn(a, b):
    return jnp.dot(a, b, preferred_element_type=F32)


def nt(a, b):
    return lax.dot_general(a, b, (((1,), (1,)), ((), ())), preferred_element_type=F32)


def kernel_of(exch, cot):
    row = lax.broadcasted_iota(jnp.int32, exch.shape, 0)
    col = lax.broadcasted_iota(jnp.int32, exch.shape, 1)
    on_diagonal = jnp.where(row == col, exch, 0.0)
    coul = jnp.sum(jnp.sum(on_diagonal, axis=0, keepdims=True), axis=1, keepdims=True)
    return (cot * jnp.where(row == col, coul - exch, -exch)).astype(BF16)


def row_groups(rows, width):
    fits = [n for n in range(1, rows + 1) if rows % n == 0 and rows // n % SUBLANES == 0]
    padded = {n: -(-n * width // LANES) * LANES / n for n in fits}
    least = min(padded.values())
    return min(n for n in fits if padded[n] <= 1.03 * least)


def half_of(half, kernel_ref, cot, chol_ref, trial_ref, hamil_ref, part_ref, packed_ref, groups):
    nocc, norb = chol_ref.shape[1:]
    width = norb // 4
    height = nocc // groups
    skew = 2 * width % LANES
    size = 2 * width + skew
    window = pl.ds(pl.multiple_of(half * (2 * width - skew), LANES), size)
    total = cot * nn(trial_ref[...].T, hamil_ref[:, window])
    for v in range(chol_ref.shape[0]):
        total += nn(kernel_ref[v], chol_ref[v, :, window])
    part_ref[:, :size] = total
    for place in range(2):

        @pl.when(half == place)
        def _():
            for q in range(2):
                left = place * skew + q * width
                for r in range(groups):
                    packed_ref[q, :, r * width : (r + 1) * width] = part_ref[
                        r * height : (r + 1) * height, left : left + width
                    ]


def crossing_kernel(groups, *refs):
    _, green_ref, chol_ref, cot_in, trial_in, hamil_in = refs[:6]
    second_ref, third_ref, kept_ref, paired_ref, kernel_ref, trial_ref, hamil_ref = refs[6:13]
    cot_ref, part_ref, packed_ref, sems = refs[13:]
    cut = second_ref.shape[0]
    cot_copy = pltpu.make_async_copy(cot_in, cot_ref, sems.at[0])
    trial_copy = pltpu.make_async_copy(trial_in, trial_ref, sems.at[1])
    hamil_copy = pltpu.make_async_copy(hamil_in, hamil_ref, sems.at[2])
    cot_copy.start()
    trial_copy.start()
    hamil_copy.start()
    vectors = chol_ref.shape[0]
    rank = lax.axis_index("chol")
    exchange = [nt(chol_ref[v], green_ref[0]) for v in range(vectors)]
    cot_copy.wait()
    cot = cot_ref[lax.axis_index("walk")]
    for v in range(vectors):
        kernel_ref[v] = kernel_of(exchange[v], cot)
    trial_copy.wait()
    hamil_copy.wait()
    half_of(
        1 - rank // 2, kernel_ref, cot, chol_ref, trial_ref, hamil_ref, part_ref, packed_ref, groups
    )
    second_ref[...] = packed_ref[rank % 2, :cut].astype(BF16)
    third_ref[...] = packed_ref[1 - rank % 2, :cut].astype(BF16)
    kept_ref[...] = packed_ref[rank % 2, cut:]
    paired_ref[...] = packed_ref[1 - rank % 2, cut:].astype(BF16)


def staying_kernel(groups, *refs):
    cot_ref, kernel_ref, chol_ref, trial_ref, hamil_ref = refs[:5]
    first_ref, own_ref, part_ref, packed_ref = refs[5:]
    rank = lax.axis_index("chol")
    cot = cot_ref[lax.axis_index("walk")]
    half_of(
        rank // 2, kernel_ref, cot, chol_ref, trial_ref, hamil_ref, part_ref, packed_ref, groups
    )
    first_ref[...] = packed_ref[1 - rank % 2].astype(BF16)
    own_ref[...] = packed_ref[rank % 2]


def half_scratch(nocc, norb, block):
    wide = -(-(norb // 2) // LANES) * LANES + LANES
    return [pltpu.VMEM((nocc, wide), F32), pltpu.VMEM((2,) + block, F32)]


def shape_of(x):
    return jax.ShapeDtypeStruct(x.shape, x.dtype)


def opening_kernel(out_ref):
    out_ref[...] = jnp.zeros_like(out_ref)


def opening(flops):
    return pl.pallas_call(
        opening_kernel,
        out_shape=jax.ShapeDtypeStruct((SUBLANES, LANES), F32),
        out_specs=pl.BlockSpec(memory_space=pltpu.VMEM),
        cost_estimate=pl.CostEstimate(flops=flops, bytes_accessed=4096, transcendentals=0),
        compiler_params=pltpu.CompilerParams(vmem_limit_bytes=MIB, has_side_effects=True),
    )()


def crossing(groups, cut, token, cot, green, chol, trial, hamil):
    _, nocc, norb = green.shape
    vectors = chol.shape[0]
    block = (nocc // groups, groups * (norb // 4))
    rest = (block[0] - cut, block[1])
    vmem = pl.BlockSpec(memory_space=pltpu.VMEM)
    loaded = [pltpu.with_memory_space_constraint(x, pltpu.HBM) for x in (cot, trial, hamil)]
    return pl.pallas_call(
        functools.partial(crossing_kernel, groups),
        out_shape=[jax.ShapeDtypeStruct((cut, block[1]), BF16)] * 2
        + [jax.ShapeDtypeStruct(rest, F32), jax.ShapeDtypeStruct(rest, BF16)]
        + [jax.ShapeDtypeStruct((vectors, nocc, nocc), BF16), shape_of(trial), shape_of(hamil)],
        in_specs=[vmem] * 3 + [pl.BlockSpec(memory_space=pltpu.HBM)] * 3,
        out_specs=[vmem] * 7,
        scratch_shapes=[pltpu.SMEM(cot.shape, F32)]
        + half_scratch(nocc, norb, block)
        + [pltpu.SemaphoreType.DMA((3,))],
        cost_estimate=pl.CostEstimate(
            flops=nocc * norb * (3 * vectors * nocc + trial.shape[0]),
            bytes_accessed=2 * (green.size + chol.size + trial.size + hamil.size),
            transcendentals=0,
        ),
        compiler_params=pltpu.CompilerParams(vmem_limit_bytes=16 * MIB),
        name="crossing",
    )(token, green, chol, *loaded)


def staying(groups, cot, kernels, chol, trial, hamil):
    vectors, nocc, norb = chol.shape
    block = (nocc // groups, groups * (norb // 4))
    vmem = pl.BlockSpec(memory_space=pltpu.VMEM)
    return pl.pallas_call(
        functools.partial(staying_kernel, groups),
        out_shape=[jax.ShapeDtypeStruct(block, BF16), jax.ShapeDtypeStruct(block, F32)],
        in_specs=[pl.BlockSpec(memory_space=pltpu.SMEM)] + [vmem] * 4,
        out_specs=[vmem] * 2,
        scratch_shapes=half_scratch(nocc, norb, block),
        cost_estimate=pl.CostEstimate(
            flops=nocc * norb * (vectors * nocc + trial.shape[0]),
            bytes_accessed=2 * (chol.size + trial.size + hamil.size),
            transcendentals=0,
        ),
        compiler_params=pltpu.CompilerParams(vmem_limit_bytes=16 * MIB),
        name="staying",
    )(cot, kernels, chol, trial, hamil)


def unpacked_rows(out_ref, packed_ref, groups):
    height, width = packed_ref.shape[0], packed_ref.shape[1] // groups
    for r in range(groups):
        out_ref[r * height : (r + 1) * height, :] = packed_ref[:, r * width : (r + 1) * width]


def share_of(green_ref, wide_ref, rank, ways):
    norb = green_ref.shape[2]
    width = norb // ways
    begin = rank * width // LANES * LANES
    size = window_size(norb, ways)
    window = pl.ds(pl.multiple_of(begin, LANES), size)
    wide_ref[:, :size] = green_ref[0, :, window].astype(F32)
    moved = pltpu.roll(wide_ref[...], wide_ref.shape[1] - (rank * width - begin), 1)
    return moved[:, :width].astype(BF16)


def window_size(norb, ways):
    width = norb // ways
    return width + max(w * width % LANES for w in range(ways))


def window_scratch(nocc, norb, ways):
    return pltpu.VMEM((nocc, -(-window_size(norb, ways) // LANES) * LANES), F32)


def call(kernel, out_shape, args, flops, moved, **more):
    vmem = pl.BlockSpec(memory_space=pltpu.VMEM)
    smem = pl.BlockSpec(memory_space=pltpu.SMEM)
    return pl.pallas_call(
        kernel,
        out_shape=out_shape,
        in_specs=[smem if x.ndim == 1 else vmem for x in args],
        cost_estimate=pl.CostEstimate(flops=flops, bytes_accessed=moved, transcendentals=0),
        compiler_params=pltpu.CompilerParams(vmem_limit_bytes=16 * MIB),
        **{"out_specs": [vmem] * len(out_shape), **more},
    )(*args)


def pair_kernel(kept_ref, received_ref, out_ref):
    out_ref[...] = (kept_ref[...] + received_ref[...].astype(F32)).astype(BF16)


def pair_sum(kept, received):
    out = [shape_of(received)]
    return call(pair_kernel, out, (kept, received), kept.size, 8 * kept.size)[0]


def early_kernel(ways, cot_ref, chol_ref, hamil_ref, green_ref, near_ref, kernel_ref, *refs):
    d_chol_ref, d_trial_ref, own_ref, near_wide = refs
    rank = lax.axis_index("walk")
    vectors = range(chol_ref.shape[0])
    flipped = [nt(near_ref[0], chol_ref[v]) for v in vectors]
    own_share = share_of(green_ref, own_ref, rank, ways)
    near_share = share_of(near_ref, near_wide, rank, ways)
    total = cot_ref[rank] * nt(hamil_ref[...], green_ref[0])
    d_trial_ref[...] = total + cot_ref[rank ^ 1] * nt(hamil_ref[...], near_ref[0])
    for v in vectors:
        own = nn(kernel_ref[v].T, own_share)
        near = kernel_of(flipped[v], cot_ref[rank ^ 1])
        d_chol_ref[v] = own + nn(near, near_share)


def middle_kernel(bits, ways, cot_ref, chol_ref, hamil_ref, green_ref, *refs):
    old_chol, old_trial, d_chol_ref, d_trial_ref, kernel_ref, wide_ref = refs
    rank = lax.axis_index("walk")
    cot = cot_ref[rank ^ bits]
    vectors = range(chol_ref.shape[0])
    flipped = [nt(green_ref[0], chol_ref[v]) for v in vectors]
    share = share_of(green_ref, wide_ref, rank, ways)
    d_trial_ref[...] = old_trial[...] + cot * nt(hamil_ref[...], green_ref[0])
    for v in vectors:
        kernel = kernel_of(flipped[v], cot)
        kernel_ref[v] = kernel
        d_chol_ref[v] = old_chol[v] + nn(kernel, share)


def trial_kernel(bits, ways, _, cot_ref, hamil_ref, green_ref, old_ref, *refs):
    d_trial_ref, share_ref, wide_ref = refs
    rank = lax.axis_index("walk")
    d_trial_ref[...] = old_ref[...] + cot_ref[rank ^ bits] * nt(hamil_ref[...], green_ref[0])
    share_ref[...] = share_of(green_ref, wide_ref, rank, ways)


def trial_term(bits, ways, token, cot, hamil, green, old):
    _, nocc, norb = green.shape
    return call(
        functools.partial(trial_kernel, bits, ways),
        [shape_of(old), jax.ShapeDtypeStruct((nocc, norb // ways), BF16)],
        (token, cot, hamil, green, old),
        2 * nocc * hamil.size,
        2 * (hamil.size + green.size),
        scratch_shapes=[window_scratch(nocc, norb, ways)],
    )


def chol_kernel(kernel_ref, share_ref, old_ref, out_ref):
    for v in range(kernel_ref.shape[0]):
        out_ref[v] = old_ref[v] + nn(kernel_ref[v], share_ref[...])


def chol_term(kernels, share, old):
    return call(
        chol_kernel,
        [shape_of(old)],
        (kernels, share, old),
        2 * kernels.size * share.shape[1],
        8 * old.size,
    )[0]


def walkers(kernel, ways, cot, chol, hamil, greens, *rest, passed=False):
    vectors, nocc, norb = chol.shape
    width = norb // ways
    return call(
        kernel,
        [
            jax.ShapeDtypeStruct((vectors, nocc, width), F32),
            jax.ShapeDtypeStruct((hamil.shape[0], nocc), F32),
        ]
        + [jax.ShapeDtypeStruct((vectors, nocc, nocc), BF16)] * passed,
        (cot, chol, hamil, *greens, *rest),
        2 * nocc * len(greens) * (nocc * vectors * (norb + width) + hamil.size),
        2 * (chol.size + len(greens) * nocc * norb),
        scratch_shapes=[window_scratch(nocc, norb, ways)] * len(greens),
    )


def joined_kernel(groups, cut, chol_ref, trial_ref, *refs):
    own_ref, first_ref, second_ref, third_ref, pair_ref = refs[:5]
    green_out, chol_out, trial_out, sum_ref, d_green, sems = refs[5:]
    chol_copy = pltpu.make_async_copy(chol_ref, chol_out, sems.at[1])
    chol_copy.start()
    trial_copy = pltpu.make_async_copy(trial_ref, trial_out, sems.at[2])
    trial_copy.start()
    total = own_ref[...] + first_ref[...].astype(F32)
    sum_ref[:cut] = total[:cut] + second_ref[...].astype(F32) + third_ref[...].astype(F32)
    sum_ref[cut:] = total[cut:] + pair_ref[...].astype(F32)
    unpacked_rows(d_green.at[0], sum_ref, groups)
    green_copy = pltpu.make_async_copy(d_green, green_out, sems.at[0])
    green_copy.start()
    chol_copy.wait()
    trial_copy.wait()
    green_copy.wait()


def joined(groups, cut, d_chol, d_trial, own, received):
    height, long = own.shape
    shape = (1, groups * height, long // groups)
    return call(
        functools.partial(joined_kernel, groups, cut),
        [jax.ShapeDtypeStruct(shape, F32), shape_of(d_chol), shape_of(d_trial)],
        (d_chol, d_trial, own, *received),
        own.size * 4,
        own.size * 16,
        out_specs=[pl.BlockSpec(memory_space=pltpu.HBM)] * 3,
        scratch_shapes=[
            pltpu.VMEM((height, long), F32),
            pltpu.VMEM(shape, F32),
            pltpu.SemaphoreType.DMA((3,)),
        ],
    )


def swapped(x, axis, bits):
    return lax.ppermute(x, axis, [(i, i ^ bits) for i in range(lax.axis_size(axis))])


def shards(green, chol, trial, hamil, energy_cot):
    ways = lax.axis_size("walk")
    _, nocc, norb = green.shape
    groups = row_groups(nocc, norb // lax.axis_size("chol"))
    cut = nocc // groups * 2 // 5 // SUBLANES * SUBLANES
    far = swapped(green, "walk", 2)
    token = opening(4 * 10**9)
    second, third, kept, paired, kernels, trial, hamil = crossing(
        groups, cut, token, energy_cot, green, chol, trial, hamil
    )
    paired = swapped(paired, "chol", 1)
    second = swapped(second, "chol", 2)
    third = swapped(third, "chol", 3)
    near = swapped(green, "walk", 1)
    both = swapped(pair_sum(kept, paired), "chol", 2)
    first, own = staying(groups, energy_cot, kernels, chol, trial, hamil)
    first = swapped(first, "chol", 1)
    early = functools.partial(early_kernel, ways)
    same = (ways, energy_cot, chol, hamil)
    sums = walkers(early, *same, [green, near], kernels)
    other = swapped(far, "walk", 1)
    middle = functools.partial(middle_kernel, 2, ways)
    d_chol, d_trial, kernels = walkers(middle, *same, [far], *sums, passed=True)
    kernels = swapped(kernels, "walk", 1)
    mark = opening(1000)
    d_trial, share = trial_term(3, ways, mark, energy_cot, hamil, other, d_trial)
    d_chol = chol_term(kernels, share, d_chol)
    received = (first, second, third, both)
    return tuple(joined(groups, cut, d_chol, d_trial, own, received))


def solution(mesh):
    fits = mesh.shape["walk"] == 4 and mesh.shape["chol"] == 4

    def body(green, *rest):
        if fits and green.shape[0] == 1 and green.shape[1] % SUBLANES == 0:
            return shards(green, *rest)
        return plain(green, *rest)

    return jax.shard_map(
        body,
        mesh=mesh,
        in_specs=(
            P(("groups", "walk"), None, None),
            P(("groups", "chol"), None, None),
            P(("groups", "chol"), None),
            P("chol", None),
            P("groups"),
        ),
        out_specs=(
            P(("groups", "walk"), None, "chol"),
            P(("groups", "chol"), None, "walk"),
            P(("groups", "chol"), None),
        ),
        check_vma=False,
    )
```
